32 devices in a mesh: wide: 8 (over z, y), narrow: 4 (over x, core).
Axes of the slice: x: 2, y: 2, z: 4, core: 2. Of those that a mesh axis runs over, the one named last changes fastest.
Arguments:
- probes: bfloat16 [32768, 256], P(('wide', 'narrow')), may hold values from -6 to 6
- leaf_basis: bfloat16 [64, 512, 256], P(('wide', 'narrow')), may hold values from -0.25 to 0.25
- transfer: bfloat16 [5, 2, 256, 256], replicated, may hold values from -0.375 to 0.375
- coupling_pool: bfloat16 [6, 3, 256, 256], replicated, may hold values from -0.375 to 0.375
- coupling_ids: int32 [126], replicated, may hold values from 0 to 2
- near_blocks: bfloat16 [64, 3, 512, 512], P(('wide', 'narrow')), may hold values from -0.25 to 0.25
- near_mask: int32 [64, 2], P(('wide', 'narrow')), may hold values 0 or 1
Outputs:
- product: bfloat16 [32768, 256], P(('wide', 'narrow'))
The draws below stay inside these ranges and needn't reach their ends.
Inputs may be any that keep to these rules, and one draw needn't show every extreme that they name: `coupling_ids`: entry 2 * 64 - 2 (64 / 2^l) + a gives the coupling block of node a of level l. `near_mask`: column 0 is the left neighbour, column 1 the right one.
All inputs are finite; a program needn't handle non-finite values. No bound on the sum of `near_mask` on one device may be relied on, other than what follows from the above.
Results may differ from the reference program's by a relative error of at most 0.018.
Values may be sent and summed in bfloat16 or wider, within the bound.
A program may use at most 64 MiB of HBM per device.

```python
import jax
import jax.numpy as jnp
from jax import lax

LEAF = 512
RANK = 256
PROBES = 256
POOL = 3
LEVELS = 6
LEAVES = 64
NODES = 126
ROWS = 32768


def with_ends(drawn, rng, smallest, largest):
    spot = [jax.random.randint(jax.random.fold_in(rng, axis), (), 0, length) for axis, length in enumerate(drawn.shape)]
    widest = drawn.shape.index(max(drawn.shape))
    next_to = spot[:widest] + [(spot[widest] + 1) % drawn.shape[widest]] + spot[widest + 1:]
    return drawn.at[tuple(spot)].set(smallest).at[tuple(next_to)].set(largest)


def shard_levels(rng, extent, shards, smallest, largest):
    factor_of = 1.0
    for axis_at, shards_of in shards:
        heights = jax.random.uniform(jax.random.fold_in(jax.random.fold_in(rng, 6), axis_at), (shards_of,), jnp.float32, smallest / len(shards), largest / len(shards))
        factor_of = factor_of * jnp.repeat(jnp.exp(heights), extent[axis_at] // shards_of).reshape((-1,) + (1,) * (len(extent) - 1 - axis_at))
    return factor_of


def scatter_about(stream_key, extent, width, most, cuts=(), held_as=jnp.bfloat16):
    drawn = jax.random.normal(stream_key, extent, jnp.float32) * width
    if len(cuts) > 0:
        drawn = shard_levels(stream_key, extent, cuts, -0.22, 0.18) * drawn
    return jnp.clip(drawn, min=-most, max=most).astype(held_as)


def setup_inputs(seed: int = 0) -> dict:
    key_list = jax.random.split(jax.random.key(seed), 8)
    probes = scatter_about(key_list[0], (ROWS, PROBES), 1.0, 6.0, ((0, 32),))
    leaf_basis = scatter_about(key_list[1], (LEAVES, LEAF, RANK), LEAF ** -0.5, 0.25, ((0, 32),))
    transfer = scatter_about(key_list[2], (LEVELS - 1, 2, RANK, RANK), RANK ** -0.5, 0.375)
    coupling_pool = scatter_about(key_list[3], (LEVELS, POOL, RANK, RANK), RANK ** -0.5, 0.375)
    coupling_ids = with_ends(jax.random.randint(key_list[4], (NODES,), 0, POOL), jax.random.fold_in(key_list[4], 1), 0, POOL - 1).astype(jnp.int32)
    near_blocks = scatter_about(key_list[5], (LEAVES, 3, LEAF, LEAF), LEAF ** -0.5, 0.25, ((0, 32),))
    near_mask = with_ends((jax.random.randint(key_list[6], (LEAVES, 2), 0, 4) < 3).astype(jnp.int32), jax.random.fold_in(key_list[6], 1), 0, 1)
    return dict(probes=probes, leaf_basis=leaf_basis, transfer=transfer, coupling_pool=coupling_pool, coupling_ids=coupling_ids, near_blocks=near_blocks, near_mask=near_mask)


half_root = 0.7071067811865476


def reference(probes, leaf_basis, transfer, coupling_pool, coupling_ids, near_blocks, near_mask):
    leaves = leaf_basis.shape[0]
    levels = leaves.bit_length() - 1
    panels = probes.reshape(leaves, LEAF, PROBES)
    block = jnp.einsum('kir,kip->krp', leaf_basis.astype(jnp.float32), panels.astype(jnp.float32)).astype(jnp.bfloat16)
    blocks = [block]
    for level in range(levels - 1):
        pairs = block.reshape(block.shape[0] // 2, 2, RANK, PROBES).astype(jnp.float32)
        left = jnp.einsum('sr,ksp->krp', transfer[level, 0].astype(jnp.float32), pairs[:, 0])
        right = jnp.einsum('sr,ksp->krp', transfer[level, 1].astype(jnp.float32), pairs[:, 1])
        block = ((left + right) * half_root).astype(jnp.bfloat16)
        blocks.append(block)
    couplings = []
    for level in range(levels):
        count = leaves >> level
        offset = 2 * leaves - 2 * count
        picks = coupling_ids[offset:offset + count]
        mats = coupling_pool[level][picks].astype(jnp.float32)
        sibling = blocks[level].reshape(count // 2, 2, RANK, PROBES)[:, ::-1].reshape(count, RANK, PROBES)
        couplings.append(jnp.einsum('krs,ksp->krp', mats, sibling.astype(jnp.float32)))
    field = couplings[levels - 1]
    for level in range(levels - 2, -1, -1):
        coarse = field.astype(jnp.bfloat16).astype(jnp.float32)
        even = jnp.einsum('rs,ksp->krp', transfer[level, 0].astype(jnp.float32), coarse)
        odd = jnp.einsum('rs,ksp->krp', transfer[level, 1].astype(jnp.float32), coarse)
        spread = jnp.stack([even, odd], axis=1).reshape(-1, RANK, PROBES)
        field = couplings[level] + spread
    far = jnp.einsum('kir,krp->kip', leaf_basis.astype(jnp.float32), field.astype(jnp.bfloat16).astype(jnp.float32))
    empty = jnp.zeros((1, LEAF, PROBES), probes.dtype)
    padded = jnp.concatenate([empty, panels, empty], axis=0)
    weights = near_mask.astype(jnp.float32)

    def near_leaf(items):
        local_blocks, before, middle, after, keep = items
        total = jnp.dot(local_blocks[0], before, preferred_element_type=jnp.float32) * keep[0]
        total = total + jnp.dot(local_blocks[1], middle, preferred_element_type=jnp.float32)
        return total + jnp.dot(local_blocks[2], after, preferred_element_type=jnp.float32) * keep[1]

    near = lax.map(near_leaf, (near_blocks, padded[:-2], padded[1:-1], padded[2:], weights))
    return (far + near).astype(jnp.bfloat16).reshape(leaves * LEAF, PROBES)
```

```python
import functools

import jax
import jax.numpy as jnp
from jax import lax
from jax.experimental import pallas as pl
from jax.experimental.pallas import tpu as pltpu
from jax.sharding import PartitionSpec as P

half_root = 0.7071067811865476
LANES = 128
ROWS = 8
NN = (((1,), (0,)), ((), ()))
NT = (((1,), (1,)), ((), ()))
TN = (((0,), (0,)), ((), ()))


def dot(a, b, dims):
    return lax.dot_general(a, b, dims, preferred_element_type=jnp.float32)


def pack(value, count):
    rows, rank = value.shape
    parts = [
        value[:, at : at + LANES].reshape(count, rows // count, LANES)
        for at in range(0, rank, LANES)
    ]
    return jnp.concatenate(parts, axis=1).astype(jnp.bfloat16)


def unpack(value, rank):
    count, rows, _ = value.shape
    k = rows * LANES // rank
    value = value.astype(jnp.float32)
    parts = [value[:, at : at + k].reshape(count * k, LANES) for at in range(0, rows, k)]
    return jnp.concatenate(parts, axis=1)


def swap_pairs(value, k):
    rows, rank = value.shape
    blocks = [value[at : at + k] for at in range(0, rows, k)]
    return jnp.concatenate([blocks[b ^ 1] for b in range(rows // k)], axis=0)


def every_other(value, k, first):
    rows, _ = value.shape
    return jnp.concatenate([value[at : at + k] for at in range(first * k, rows, 2 * k)], axis=0)


def interleave(even, odd, k):
    rows, _ = even.shape
    blocks = []
    for at in range(0, rows, k):
        blocks += [even[at : at + k], odd[at : at + k]]
    return jnp.concatenate(blocks, axis=0)


def kernel(
    n_wide, n_narrow, group, extra,
    ids, mask, probes, basis, transfer, pool, near, out,
    xv, bv, tv, p_own, pv, nv, halo, acc, coef, loc, send1, recv1, send2, recv2, outer_send, outer_recv,
    load_sem, pair_sem, halo_send, halo_recv, outer_sems,
):
    n = n_wide * n_narrow
    leaf_dev, leaf_rows, rank = bv.shape
    width = xv.shape[1]
    k = width // group
    choices = pv.shape[1]
    local_bits = leaf_dev.bit_length() - 1
    group_bits = group.bit_length() - 1
    levels = local_bits + group_bits + extra
    leaves = leaf_dev * n

    me = lax.axis_index("wide") * n_narrow + lax.axis_index("narrow")
    mine = me % group
    base = me - mine

    def place(device):
        return (device // n_narrow, device % n_narrow)

    def outer_partner(e):
        stride = group << e
        return me + (1 - 2 * ((me // stride) % 2)) * stride

    def id_at(level, node):
        return ids[2 * leaves - 2 * (leaves >> level) + node]

    loads = {}

    def load(name, src, dst):
        copy = pltpu.make_async_copy(src, dst, load_sem.at[len(loads)])
        copy.start()
        loads[name] = copy

    for i in range(leaf_dev):
        panel = pl.ds(i * leaf_rows, leaf_rows)
        load(("x", i), probes.at[panel], xv.at[panel])
        load(("b", i), basis.at[i], bv.at[i])
    low = pl.ds(0, local_bits)
    high_t = pl.ds(local_bits, levels - 1 - local_bits)
    high_p = pl.ds(local_bits, levels - local_bits)
    load("t_low", transfer.at[low], tv.at[low])
    load("t_high", transfer.at[high_t], tv.at[high_t])
    load("p_high", pool.at[high_p], pv.at[high_p])
    load("p_low", pool.at[low], p_own)
    for i in range(leaf_dev):
        load(("n", i), near.at[i], nv.at[i])

    barrier = pltpu.get_barrier_semaphore()

    def greet(device):
        pl.semaphore_signal(
            barrier, inc=1, device_id=place(device), device_id_type=pl.DeviceIdType.MESH
        )

    for s in range(1, group):
        greet(base + (mine + s) % group)
    expected = group - 1
    if extra:
        for e in range(extra):
            greet(outer_partner(e))
        up = jnp.logical_and(mine == group - 1, me < n - 1)
        down = jnp.logical_and(mine == 0, me > 0)
        pl.when(up)(lambda: greet(me + 1))
        pl.when(down)(lambda: greet(me - 1))
        expected = expected + extra + jnp.where(up, 1, 0) + jnp.where(down, 1, 0)

    def panel_of(i):
        return xv[i * leaf_rows : (i + 1) * leaf_rows, :]

    current = []
    for i in range(leaf_dev):
        loads["x", i].wait()
        loads["b", i].wait()
        current.append(dot(panel_of(i), bv[i], TN).astype(jnp.bfloat16))
    loads["t_low"].wait()
    at = 0
    starts = []
    for level in range(local_bits):
        starts.append(at)
        for value in current:
            coef[at] = value
            at += 1
        lifted = [
            (dot(current[2 * a], tv[level, 0], NN) + dot(current[2 * a + 1], tv[level, 1], NN))
            * half_root
            for a in range(len(current) // 2)
        ]
        current = [value.astype(jnp.bfloat16) for value in lifted]
    send1[...] = pack(lifted[0], group)
    recv1[pl.ds(mine, 1)] = send1[pl.ds(mine, 1)]

    pl.semaphore_wait(barrier, expected)

    def spread(send, recv, sems):
        for s in range(1, group):
            to = (mine + s) % group
            pltpu.make_async_remote_copy(
                src_ref=send.at[to],
                dst_ref=recv.at[mine],
                send_sem=pair_sem.at[sems],
                recv_sem=pair_sem.at[sems + 1],
                device_id=place(base + to),
                device_id_type=pl.DeviceIdType.MESH,
            ).start()

    def settle(ref, sem):
        most = ref.at[pl.ds(0, group - 1)]
        pltpu.make_async_copy(most, most, pair_sem.at[sem]).wait()

    spread(send1, recv1, 0)

    def halo_copy(side):
        first = (leaf_dev - 1) * leaf_rows if side == 0 else 0
        return pltpu.make_async_remote_copy(
            src_ref=xv.at[pl.ds(first, leaf_rows)],
            dst_ref=halo.at[side],
            send_sem=halo_send.at[side],
            recv_sem=halo_recv.at[side],
            device_id=place(me + 1 if side == 0 else me - 1),
            device_id_type=pl.DeviceIdType.MESH,
        )

    not_last = me < n - 1
    not_first = me > 0
    pl.when(not_last)(lambda: halo_copy(0).start())
    pl.when(not_first)(lambda: halo_copy(1).start())

    @pl.when(me == 0)
    def _():
        halo[0] = jnp.zeros_like(halo[0])

    @pl.when(me == n - 1)
    def _():
        halo[1] = jnp.zeros_like(halo[1])

    loads["p_low"].wait()
    for level in range(local_bits):
        count = leaf_dev >> level
        for a in range(count):
            matrix = p_own[level, id_at(level, me * count + a)]
            loc[starts[level] + a] = dot(coef[starts[level] + (a ^ 1)], matrix, NT)
    for i in range(leaf_dev):
        loads["n", i].wait()
        total = dot(nv[i, 1], panel_of(i), NN)
        if i > 0:
            total += dot(nv[i, 0], panel_of(i - 1), NN) * mask[i, 0].astype(jnp.float32)
        if i < leaf_dev - 1:
            total += dot(nv[i, 2], panel_of(i + 1), NN) * mask[i, 1].astype(jnp.float32)
        acc[i * leaf_rows : (i + 1) * leaf_rows, :] = total
    loads["t_high"].wait()
    loads["p_high"].wait()

    settle(recv1, 1)

    def coupled(value, level, first, count):
        chosen = jnp.concatenate(
            [jnp.full((k, rank), id_at(level, first + (b ^ 1)), jnp.int32) for b in range(count)],
            axis=0,
        )
        total = None
        for q in range(choices):
            part = jnp.where(chosen == q, value, 0.0).astype(jnp.bfloat16)
            part = dot(part, pv[level, q], NT)
            total = part if total is None else total + part
        return swap_pairs(total, k)

    value = unpack(recv1[...], rank)
    couplings = []
    for j in range(group_bits):
        level = local_bits + j
        count = group >> j
        couplings.append(coupled(value, level, base >> j, count))
        if level < levels - 1:
            left = every_other(value, k, 0).astype(jnp.bfloat16)
            right = every_other(value, k, 1).astype(jnp.bfloat16)
            value = (dot(left, tv[level, 0], NN) + dot(right, tv[level, 1], NN)) * half_root
            value = value.astype(jnp.bfloat16).astype(jnp.float32)
    outer = []
    for e in range(extra):
        level = local_bits + group_bits + e
        bit = (me // (group << e)) % 2
        outer_send[e] = pack(value, 1)[0]
        copy = pltpu.make_async_remote_copy(
            src_ref=outer_send.at[e],
            dst_ref=outer_recv.at[e],
            send_sem=outer_sems.at[0, e],
            recv_sem=outer_sems.at[1, e],
            device_id=place(outer_partner(e)),
            device_id_type=pl.DeviceIdType.MESH,
        )
        copy.start()
        copy.wait()
        other = unpack(outer_recv[e][None], rank)
        matrix = pv[level, id_at(level, me // (group << e))]
        outer.append(dot(other.astype(jnp.bfloat16), matrix, NT))
        if level < levels - 1:
            own = dot(value.astype(jnp.bfloat16), tv[level, bit], NN)
            value = (own + dot(other.astype(jnp.bfloat16), tv[level, 1 - bit], NN)) * half_root
            value = value.astype(jnp.bfloat16).astype(jnp.float32)

    field = None
    for e in reversed(range(extra)):
        level = local_bits + group_bits + e
        bit = (me // (group << e)) % 2
        below = outer[e]
        if field is not None:
            below += dot(field.astype(jnp.bfloat16), tv[level, bit], NT)
        field = below
    for j in reversed(range(group_bits)):
        level = local_bits + j
        below = couplings[j]
        if field is not None:
            coarse = field.astype(jnp.bfloat16)
            below += interleave(dot(coarse, tv[level, 0], NT), dot(coarse, tv[level, 1], NT), k)
        field = below
    send2[...] = pack(field, group)
    recv2[pl.ds(mine, 1)] = send2[pl.ds(mine, 1)]
    spread(send2, recv2, 2)

    pl.when(not_first)(lambda: halo_copy(0).wait_recv())
    first = pl.ds(0, leaf_rows)
    acc[first, :] += dot(nv[0, 0], halo[0], NN) * mask[0, 0].astype(jnp.float32)
    pl.when(not_last)(lambda: halo_copy(1).wait_recv())
    last = pl.ds((leaf_dev - 1) * leaf_rows, leaf_rows)
    acc[last, :] += dot(nv[leaf_dev - 1, 2], halo[1], NN) * mask[leaf_dev - 1, 1].astype(
        jnp.float32
    )

    settle(recv2, 3)
    fields = [unpack(recv2[...], rank).astype(jnp.bfloat16)]
    for level in reversed(range(local_bits)):
        fields = [
            (loc[starts[level] + a] + dot(fields[a // 2], tv[level, a % 2], NT)).astype(
                jnp.bfloat16
            )
            for a in range(leaf_dev >> level)
        ]
    for i in range(leaf_dev):
        rows = pl.ds(i * leaf_rows, leaf_rows)
        out[rows, :] = (acc[rows, :] + dot(bv[i], fields[i], NT)).astype(out.dtype)

    settle(send1, 0)
    settle(send2, 2)
    pl.when(not_last)(lambda: halo_copy(0).wait_send())
    pl.when(not_first)(lambda: halo_copy(1).wait_send())


def on_device(probes, leaf_basis, transfer, coupling_pool, coupling_ids, near_blocks, near_mask):
    leaf_dev, leaf_rows, rank = leaf_basis.shape
    width = probes.shape[1]
    n_narrow = lax.axis_size("narrow")
    n_wide = lax.axis_size("wide")
    n = n_narrow * n_wide
    group = min(n, width // ROWS)
    extra = (n // group).bit_length() - 1
    panel = (width // group) * rank // LANES
    bf16, f32 = jnp.bfloat16, jnp.float32
    anywhere = pl.BlockSpec(memory_space=pltpu.HBM)
    scalars = pl.BlockSpec(memory_space=pltpu.SMEM)
    slots = pltpu.VMEM((group, panel, LANES), bf16)
    outer = pltpu.VMEM((max(extra, 1), panel, LANES), bf16)
    dma = pltpu.SemaphoreType.DMA
    return pl.pallas_call(
        functools.partial(kernel, n_wide, n_narrow, group, extra),
        out_shape=jax.ShapeDtypeStruct(probes.shape, bf16),
        in_specs=[scalars, scalars] + [anywhere] * 5,
        out_specs=pl.BlockSpec(memory_space=pltpu.VMEM),
        scratch_shapes=[
            pltpu.VMEM(probes.shape, bf16),
            pltpu.VMEM(leaf_basis.shape, bf16),
            pltpu.VMEM(transfer.shape, bf16),
            pltpu.VMEM((leaf_dev.bit_length() - 1,) + coupling_pool.shape[1:], bf16),
            pltpu.VMEM(coupling_pool.shape, bf16),
            pltpu.VMEM(near_blocks.shape, bf16),
            pltpu.VMEM((2, leaf_rows, width), bf16),
            pltpu.VMEM(probes.shape, f32),
            pltpu.VMEM((2 * leaf_dev - 2, width, rank), bf16),
            pltpu.VMEM((2 * leaf_dev - 2, width, rank), f32),
            slots, slots, slots, slots, outer, outer,
            dma((3 * leaf_dev + 4,)),
            dma((4,)),
            dma((2,)),
            dma((2,)),
            dma((2, max(extra, 1))),
        ],
        compiler_params=pltpu.CompilerParams(
            collective_id=0, has_side_effects=True, vmem_limit_bytes=60 * 1024 * 1024
        ),
    )(coupling_ids, near_mask, probes, leaf_basis, transfer, coupling_pool, near_blocks)


def solution(mesh):
    in_specs = (
        P(("wide", "narrow"), None),
        P(("wide", "narrow"), None, None),
        P(),
        P(),
        P(),
        P(("wide", "narrow"), None, None, None),
        P(("wide", "narrow"), None),
    )
    return jax.shard_map(
        on_device,
        mesh=mesh,
        in_specs=in_specs,
        out_specs=P(("wide", "narrow"), None),
        check_vma=False,
    )
```

```python
import functools

import jax
import jax.numpy as jnp
from jax import lax
from jax.experimental import pallas as pl
from jax.experimental.pallas import tpu as pltpu
from jax.sharding import PartitionSpec as P

half_root = 0.7071067811865476
LANES = 128
ROWS = 8
NN = (((1,), (0,)), ((), ()))
NT = (((1,), (1,)), ((), ()))
TN = (((0,), (0,)), ((), ()))


def dot(a, b, dims):
    return lax.dot_general(a, b, dims, preferred_element_type=jnp.float32)


def pack(value, count):
    rows, rank = value.shape
    parts = [
        value[:, at : at + LANES].reshape(count, rows // count, LANES)
        for at in range(0, rank, LANES)
    ]
    return jnp.concatenate(parts, axis=1).astype(jnp.bfloat16)


def unpack(value, rank):
    count, rows, _ = value.shape
    k = rows * LANES // rank
    value = value.astype(jnp.float32)
    parts = [value[:, at : at + k].reshape(count * k, LANES) for at in range(0, rows, k)]
    return jnp.concatenate(parts, axis=1)


def swap_pairs(value, k):
    rows, rank = value.shape
    blocks = [value[at : at + k] for at in range(0, rows, k)]
    return jnp.concatenate([blocks[b ^ 1] for b in range(rows // k)], axis=0)


def every_other(value, k, first):
    rows, _ = value.shape
    return jnp.concatenate([value[at : at + k] for at in range(first * k, rows, 2 * k)], axis=0)


def interleave(even, odd, k):
    rows, _ = even.shape
    blocks = []
    for at in range(0, rows, k):
        blocks += [even[at : at + k], odd[at : at + k]]
    return jnp.concatenate(blocks, axis=0)


def kernel(
    n_wide, n_narrow, group, extra,
    ids_hbm, mask_hbm, probes, basis, transfer, pool, near, out,
    ids, mask, xv, bv, tv, p_own, pv, nv, halo, acc, coef, loc, send1, recv1, send2, recv2, outer_send, outer_recv,
    load_sem, pair_sem, halo_send, halo_recv, outer_sems,
):
    n = n_wide * n_narrow
    leaf_dev, leaf_rows, rank = bv.shape
    width = xv.shape[1]
    k = width // group
    choices = pv.shape[1]
    local_bits = leaf_dev.bit_length() - 1
    group_bits = group.bit_length() - 1
    levels = local_bits + group_bits + extra
    leaves = leaf_dev * n

    me = lax.axis_index("wide") * n_narrow + lax.axis_index("narrow")
    mine = me % group
    base = me - mine

    def place(device):
        return (device // n_narrow, device % n_narrow)

    def outer_partner(e):
        stride = group << e
        return me + (1 - 2 * ((me // stride) % 2)) * stride

    def id_at(level, node):
        return ids[2 * leaves - 2 * (leaves >> level) + node]

    loads = {}

    def load(name, src, dst):
        copy = pltpu.make_async_copy(src, dst, load_sem.at[len(loads)])
        copy.start()
        loads[name] = copy

    for i in range(leaf_dev):
        panel = pl.ds(i * leaf_rows, leaf_rows)
        load(("x", i), probes.at[panel], xv.at[panel])
        load(("b", i), basis.at[i], bv.at[i])
    low = pl.ds(0, local_bits)
    high_t = pl.ds(local_bits, levels - 1 - local_bits)
    high_p = pl.ds(local_bits, levels - local_bits)
    load("t_low", transfer.at[low], tv.at[low])
    load("ids", ids_hbm, ids)
    load("mask", mask_hbm, mask)
    load("t_high", transfer.at[high_t], tv.at[high_t])
    load("p_high", pool.at[high_p], pv.at[high_p])
    load("p_low", pool.at[low], p_own)
    for i in range(leaf_dev):
        load(("n", i), near.at[i], nv.at[i])

    barrier = pltpu.get_barrier_semaphore()

    def greet(device):
        pl.semaphore_signal(
            barrier, inc=1, device_id=place(device), device_id_type=pl.DeviceIdType.MESH
        )

    for s in range(1, group):
        greet(base + (mine + s) % group)
    expected = group - 1
    if extra:
        for e in range(extra):
            greet(outer_partner(e))
        up = jnp.logical_and(mine == group - 1, me < n - 1)
        down = jnp.logical_and(mine == 0, me > 0)
        pl.when(up)(lambda: greet(me + 1))
        pl.when(down)(lambda: greet(me - 1))
        expected = expected + extra + jnp.where(up, 1, 0) + jnp.where(down, 1, 0)

    def panel_of(i):
        return xv[i * leaf_rows : (i + 1) * leaf_rows, :]

    current = []
    for i in range(leaf_dev):
        loads["x", i].wait()
        loads["b", i].wait()
        current.append(dot(panel_of(i), bv[i], TN).astype(jnp.bfloat16))
    loads["t_low"].wait()
    at = 0
    starts = []
    for level in range(local_bits):
        starts.append(at)
        for value in current:
            coef[at] = value
            at += 1
        lifted = [
            (dot(current[2 * a], tv[level, 0], NN) + dot(current[2 * a + 1], tv[level, 1], NN))
            * half_root
            for a in range(len(current) // 2)
        ]
        current = [value.astype(jnp.bfloat16) for value in lifted]
    send1[...] = pack(lifted[0], group)
    recv1[pl.ds(mine, 1)] = send1[pl.ds(mine, 1)]

    pl.semaphore_wait(barrier, expected)

    def spread(send, recv, sems):
        for s in range(1, group):
            to = (mine + s) % group
            pltpu.make_async_remote_copy(
                src_ref=send.at[to],
                dst_ref=recv.at[mine],
                send_sem=pair_sem.at[sems],
                recv_sem=pair_sem.at[sems + 1],
                device_id=place(base + to),
                device_id_type=pl.DeviceIdType.MESH,
            ).start()

    def settle(ref, sem):
        most = ref.at[pl.ds(0, group - 1)]
        pltpu.make_async_copy(most, most, pair_sem.at[sem]).wait()

    spread(send1, recv1, 0)

    def halo_copy(side):
        first = (leaf_dev - 1) * leaf_rows if side == 0 else 0
        return pltpu.make_async_remote_copy(
            src_ref=xv.at[pl.ds(first, leaf_rows)],
            dst_ref=halo.at[side],
            send_sem=halo_send.at[side],
            recv_sem=halo_recv.at[side],
            device_id=place(me + 1 if side == 0 else me - 1),
            device_id_type=pl.DeviceIdType.MESH,
        )

    not_last = me < n - 1
    not_first = me > 0
    pl.when(not_last)(lambda: halo_copy(0).start())
    pl.when(not_first)(lambda: halo_copy(1).start())

    @pl.when(me == 0)
    def _():
        halo[0] = jnp.zeros_like(halo[0])

    @pl.when(me == n - 1)
    def _():
        halo[1] = jnp.zeros_like(halo[1])

    loads["p_low"].wait()
    loads["ids"].wait()
    loads["mask"].wait()
    for level in range(local_bits):
        count = leaf_dev >> level
        for a in range(count):
            matrix = p_own[level, id_at(level, me * count + a)]
            loc[starts[level] + a] = dot(coef[starts[level] + (a ^ 1)], matrix, NT)
    for i in range(leaf_dev):
        loads["n", i].wait()
        total = dot(nv[i, 1], panel_of(i), NN)
        if i > 0:
            total += dot(nv[i, 0], panel_of(i - 1), NN) * mask[i, 0].astype(jnp.float32)
        if i < leaf_dev - 1:
            total += dot(nv[i, 2], panel_of(i + 1), NN) * mask[i, 1].astype(jnp.float32)
        acc[i * leaf_rows : (i + 1) * leaf_rows, :] = total
    loads["t_high"].wait()
    loads["p_high"].wait()

    settle(recv1, 1)

    def coupled(value, level, first, count):
        chosen = jnp.concatenate(
            [jnp.full((k, rank), id_at(level, first + (b ^ 1)), jnp.int32) for b in range(count)],
            axis=0,
        )
        total = None
        for q in range(choices):
            part = jnp.where(chosen == q, value, 0.0).astype(jnp.bfloat16)
            part = dot(part, pv[level, q], NT)
            total = part if total is None else total + part
        return swap_pairs(total, k)

    value = unpack(recv1[...], rank)
    couplings = []
    for j in range(group_bits):
        level = local_bits + j
        count = group >> j
        couplings.append(coupled(value, level, base >> j, count))
        if level < levels - 1:
            left = every_other(value, k, 0).astype(jnp.bfloat16)
            right = every_other(value, k, 1).astype(jnp.bfloat16)
            value = (dot(left, tv[level, 0], NN) + dot(right, tv[level, 1], NN)) * half_root
            value = value.astype(jnp.bfloat16).astype(jnp.float32)
    outer = []
    for e in range(extra):
        level = local_bits + group_bits + e
        bit = (me // (group << e)) % 2
        outer_send[e] = pack(value, 1)[0]
        copy = pltpu.make_async_remote_copy(
            src_ref=outer_send.at[e],
            dst_ref=outer_recv.at[e],
            send_sem=outer_sems.at[0, e],
            recv_sem=outer_sems.at[1, e],
            device_id=place(outer_partner(e)),
            device_id_type=pl.DeviceIdType.MESH,
        )
        copy.start()
        copy.wait()
        other = unpack(outer_recv[e][None], rank)
        matrix = pv[level, id_at(level, me // (group << e))]
        outer.append(dot(other.astype(jnp.bfloat16), matrix, NT))
        if level < levels - 1:
            own = dot(value.astype(jnp.bfloat16), tv[level, bit], NN)
            value = (own + dot(other.astype(jnp.bfloat16), tv[level, 1 - bit], NN)) * half_root
            value = value.astype(jnp.bfloat16).astype(jnp.float32)

    field = None
    for e in reversed(range(extra)):
        level = local_bits + group_bits + e
        bit = (me // (group << e)) % 2
        below = outer[e]
        if field is not None:
            below += dot(field.astype(jnp.bfloat16), tv[level, bit], NT)
        field = below
    for j in reversed(range(group_bits)):
        level = local_bits + j
        below = couplings[j]
        if field is not None:
            coarse = field.astype(jnp.bfloat16)
            below += interleave(dot(coarse, tv[level, 0], NT), dot(coarse, tv[level, 1], NT), k)
        field = below
    send2[...] = pack(field, group)
    recv2[pl.ds(mine, 1)] = send2[pl.ds(mine, 1)]
    spread(send2, recv2, 2)

    pl.when(not_first)(lambda: halo_copy(0).wait_recv())
    first = pl.ds(0, leaf_rows)
    acc[first, :] += dot(nv[0, 0], halo[0], NN) * mask[0, 0].astype(jnp.float32)
    pl.when(not_last)(lambda: halo_copy(1).wait_recv())
    last = pl.ds((leaf_dev - 1) * leaf_rows, leaf_rows)
    acc[last, :] += dot(nv[leaf_dev - 1, 2], halo[1], NN) * mask[leaf_dev - 1, 1].astype(
        jnp.float32
    )

    settle(recv2, 3)
    fields = [unpack(recv2[...], rank).astype(jnp.bfloat16)]
    for level in reversed(range(local_bits)):
        fields = [
            (loc[starts[level] + a] + dot(fields[a // 2], tv[level, a % 2], NT)).astype(
                jnp.bfloat16
            )
            for a in range(leaf_dev >> level)
        ]
    for i in range(leaf_dev):
        rows = pl.ds(i * leaf_rows, leaf_rows)
        out[rows, :] = (acc[rows, :] + dot(bv[i], fields[i], NT)).astype(out.dtype)

    settle(send1, 0)
    settle(send2, 2)
    pl.when(not_last)(lambda: halo_copy(0).wait_send())
    pl.when(not_first)(lambda: halo_copy(1).wait_send())


def on_device(probes, leaf_basis, transfer, coupling_pool, coupling_ids, near_blocks, near_mask):
    leaf_dev, leaf_rows, rank = leaf_basis.shape
    width = probes.shape[1]
    n_narrow = lax.axis_size("narrow")
    n_wide = lax.axis_size("wide")
    n = n_narrow * n_wide
    group = min(n, width // ROWS)
    extra = (n // group).bit_length() - 1
    panel = (width // group) * rank // LANES
    bf16, f32 = jnp.bfloat16, jnp.float32
    arrays = (
        coupling_ids, near_mask, probes, leaf_basis, transfer, coupling_pool, near_blocks,
    )
    anywhere = pl.BlockSpec(memory_space=pltpu.HBM)
    slots = pltpu.VMEM((group, panel, LANES), bf16)
    outer = pltpu.VMEM((max(extra, 1), panel, LANES), bf16)
    dma = pltpu.SemaphoreType.DMA
    return pl.pallas_call(
        functools.partial(kernel, n_wide, n_narrow, group, extra),
        out_shape=pltpu.VMEM(probes.shape, bf16),
        in_specs=[anywhere] * 7,
        out_specs=pl.BlockSpec(memory_space=pltpu.VMEM),
        scratch_shapes=[
            pltpu.SMEM(coupling_ids.shape, jnp.int32),
            pltpu.SMEM(near_mask.shape, jnp.int32),
            pltpu.VMEM(probes.shape, bf16),
            pltpu.VMEM(leaf_basis.shape, bf16),
            pltpu.VMEM(transfer.shape, bf16),
            pltpu.VMEM((leaf_dev.bit_length() - 1,) + coupling_pool.shape[1:], bf16),
            pltpu.VMEM(coupling_pool.shape, bf16),
            pltpu.VMEM(near_blocks.shape, bf16),
            pltpu.VMEM((2, leaf_rows, width), bf16),
            pltpu.VMEM(probes.shape, f32),
            pltpu.VMEM((2 * leaf_dev - 2, width, rank), bf16),
            pltpu.VMEM((2 * leaf_dev - 2, width, rank), f32),
            slots, slots, slots, slots, outer, outer,
            dma((3 * leaf_dev + 6,)),
            dma((4,)),
            dma((2,)),
            dma((2,)),
            dma((2, max(extra, 1))),
        ],
        compiler_params=pltpu.CompilerParams(
            collective_id=0, has_side_effects=True, vmem_limit_bytes=32 * 1024 * 1024
        ),
    )(*[pltpu.with_memory_space_constraint(array, pltpu.HBM) for array in arrays])


def solution(mesh):
    in_specs = (
        P(("wide", "narrow"), None),
        P(("wide", "narrow"), None, None),
        P(),
        P(),
        P(),
        P(("wide", "narrow"), None, None, None),
        P(("wide", "narrow"), None),
    )
    return jax.shard_map(
        on_device,
        mesh=mesh,
        in_specs=in_specs,
        out_specs=P(("wide", "narrow"), None),
        check_vma=False,
    )
```

```python
import functools

import jax
import jax.numpy as jnp
from jax import lax
from jax.experimental import pallas as pl
from jax.experimental.pallas import tpu as pltpu
from jax.sharding import PartitionSpec as P

half_root = 0.7071067811865476
LANES = 128
ROWS = 8
NN = (((1,), (0,)), ((), ()))
NT = (((1,), (1,)), ((), ()))
TN = (((0,), (0,)), ((), ()))


def dot(a, b, dims):
    return lax.dot_general(a, b, dims, preferred_element_type=jnp.float32)


def pack(value, count):
    rows, rank = value.shape
    parts = [
        value[:, at : at + LANES].reshape(count, rows // count, LANES)
        for at in range(0, rank, LANES)
    ]
    return jnp.concatenate(parts, axis=1).astype(jnp.bfloat16)


def unpack(value, rank):
    count, rows, _ = value.shape
    k = rows * LANES // rank
    value = value.astype(jnp.float32)
    parts = [value[:, at : at + k].reshape(count * k, LANES) for at in range(0, rows, k)]
    return jnp.concatenate(parts, axis=1)


def swap_pairs(value, k):
    rows, rank = value.shape
    blocks = [value[at : at + k] for at in range(0, rows, k)]
    return jnp.concatenate([blocks[b ^ 1] for b in range(rows // k)], axis=0)


def every_other(value, k, first):
    rows, _ = value.shape
    return jnp.concatenate([value[at : at + k] for at in range(first * k, rows, 2 * k)], axis=0)


def interleave(even, odd, k):
    rows, _ = even.shape
    blocks = []
    for at in range(0, rows, k):
        blocks += [even[at : at + k], odd[at : at + k]]
    return jnp.concatenate(blocks, axis=0)


def kernel(
    n_wide, n_narrow, group, extra,
    ids_hbm, mask_hbm, probes, basis, transfer, pool, near, out,
    ids, mask, xv, bv, tv, p_own, pv, nv, halo, acc, coef, loc, send1, recv1, send2, recv2, outer_send, outer_recv,
    load_sem, pair_sem, halo_send, halo_recv, outer_sems,
):
    n = n_wide * n_narrow
    leaf_dev, leaf_rows, rank = bv.shape
    width = xv.shape[1]
    k = width // group
    choices = pv.shape[1]
    local_bits = leaf_dev.bit_length() - 1
    group_bits = group.bit_length() - 1
    levels = local_bits + group_bits + extra
    leaves = leaf_dev * n

    wide, narrow = lax.axis_index("wide"), lax.axis_index("narrow")
    me = wide * n_narrow + narrow
    group_wide = group // n_narrow
    wide_base = wide // group_wide * group_wide if extra else 0
    base = wide_base * n_narrow
    mine = me - base

    def place(device):
        return (device // n_narrow, device % n_narrow)

    def turned(position, step, count):
        moved = position + step
        return jnp.where(moved >= count, moved - count, moved) if step else position

    turns_narrow = []
    for step in range(n_narrow):
        moved = narrow + step
        carried = moved >= n_narrow
        turns_narrow.append((jnp.where(carried, moved - n_narrow, moved), carried))
    turns_wide = [
        turned(wide - wide_base, step % group_wide, group_wide) for step in range(group_wide + 1)
    ]
    others = []
    for step in range(1, group):
        to_narrow, carried = turns_narrow[step % n_narrow]
        at = step // n_narrow
        to_wide = jnp.where(carried, turns_wide[at + 1], turns_wide[at])
        others.append((wide_base + to_wide, to_narrow, to_wide * n_narrow + to_narrow))

    def outer_partner(e):
        stride = group << e
        return me + (1 - 2 * ((me // stride) % 2)) * stride

    def id_at(level, node):
        return ids[2 * leaves - 2 * (leaves >> level) + node]

    loads = {}

    def load(name, src, dst):
        copy = pltpu.make_async_copy(src, dst, load_sem.at[len(loads)])
        copy.start()
        loads[name] = copy

    for i in range(leaf_dev):
        panel = pl.ds(i * leaf_rows, leaf_rows)
        load(("x", i), probes.at[panel], xv.at[panel])
        load(("b", i), basis.at[i], bv.at[i])
    low = pl.ds(0, local_bits)
    high_t = pl.ds(local_bits, levels - 1 - local_bits)
    high_p = pl.ds(local_bits, levels - local_bits)
    load("t_low", transfer.at[low], tv.at[low])
    load("ids", ids_hbm, ids)
    load("mask", mask_hbm, mask)
    load("t_high", transfer.at[high_t], tv.at[high_t])
    load("p_high", pool.at[high_p], pv.at[high_p])
    load("p_low", pool.at[low], p_own)
    for i in range(leaf_dev):
        load(("n", i), near.at[i], nv.at[i])

    barrier = pltpu.get_barrier_semaphore()

    def greet(device_id):
        pl.semaphore_signal(
            barrier, inc=1, device_id=device_id, device_id_type=pl.DeviceIdType.MESH
        )

    for to_wide, to_narrow, _ in others:
        greet((to_wide, to_narrow))
    expected = group - 1
    if extra:
        for e in range(extra):
            greet(place(outer_partner(e)))
        up = jnp.logical_and(mine == group - 1, me < n - 1)
        down = jnp.logical_and(mine == 0, me > 0)
        pl.when(up)(lambda: greet(place(me + 1)))
        pl.when(down)(lambda: greet(place(me - 1)))
        expected = expected + extra + jnp.where(up, 1, 0) + jnp.where(down, 1, 0)

    def panel_of(i):
        return xv[i * leaf_rows : (i + 1) * leaf_rows, :]

    current = []
    for i in range(leaf_dev):
        loads["x", i].wait()
        loads["b", i].wait()
        current.append(dot(panel_of(i), bv[i], TN).astype(jnp.bfloat16))
    loads["t_low"].wait()
    at = 0
    starts = []
    for level in range(local_bits):
        starts.append(at)
        for value in current:
            coef[at] = value
            at += 1
        lifted = [
            (dot(current[2 * a], tv[level, 0], NN) + dot(current[2 * a + 1], tv[level, 1], NN))
            * half_root
            for a in range(len(current) // 2)
        ]
        current = [value.astype(jnp.bfloat16) for value in lifted]
    send1[...] = pack(lifted[0], group)
    recv1[pl.ds(mine, 1)] = send1[pl.ds(mine, 1)]

    loads["p_low"].wait()
    loads["ids"].wait()
    loads["mask"].wait()
    for level in range(local_bits):
        count = leaf_dev >> level
        for a in range(count):
            matrix = p_own[level, id_at(level, me * count + a)]
            loc[starts[level] + a] = dot(coef[starts[level] + (a ^ 1)], matrix, NT)
    for i in range(leaf_dev):
        loads["n", i].wait()
        total = dot(nv[i, 1], panel_of(i), NN)
        if i > 0:
            total += dot(nv[i, 0], panel_of(i - 1), NN) * mask[i, 0].astype(jnp.float32)
        if i < leaf_dev - 1:
            total += dot(nv[i, 2], panel_of(i + 1), NN) * mask[i, 1].astype(jnp.float32)
        acc[i * leaf_rows : (i + 1) * leaf_rows, :] = total
    pl.semaphore_wait(barrier, expected)

    def spread(send, recv, sems):
        for to_wide, to_narrow, to in others:
            pltpu.make_async_remote_copy(
                src_ref=send.at[to],
                dst_ref=recv.at[mine],
                send_sem=pair_sem.at[sems],
                recv_sem=pair_sem.at[sems + 1],
                device_id=(to_wide, to_narrow),
                device_id_type=pl.DeviceIdType.MESH,
            ).start()

    def settle(ref, sem):
        most = ref.at[pl.ds(0, group - 1)]
        pltpu.make_async_copy(most, most, pair_sem.at[sem]).wait()

    spread(send1, recv1, 0)

    def halo_copy(side):
        first = (leaf_dev - 1) * leaf_rows if side == 0 else 0
        return pltpu.make_async_remote_copy(
            src_ref=xv.at[pl.ds(first, leaf_rows)],
            dst_ref=halo.at[side],
            send_sem=halo_send.at[side],
            recv_sem=halo_recv.at[side],
            device_id=place(me + 1 if side == 0 else me - 1),
            device_id_type=pl.DeviceIdType.MESH,
        )

    not_last = me < n - 1
    not_first = me > 0
    pl.when(not_last)(lambda: halo_copy(0).start())
    pl.when(not_first)(lambda: halo_copy(1).start())

    @pl.when(me == 0)
    def _():
        halo[0] = jnp.zeros_like(halo[0])

    @pl.when(me == n - 1)
    def _():
        halo[1] = jnp.zeros_like(halo[1])

    loads["t_high"].wait()
    loads["p_high"].wait()

    settle(recv1, 1)

    def coupled(value, level, first, count):
        chosen = jnp.concatenate(
            [jnp.full((k, rank), id_at(level, first + (b ^ 1)), jnp.int32) for b in range(count)],
            axis=0,
        )
        total = None
        for q in range(choices):
            part = jnp.where(chosen == q, value, 0.0).astype(jnp.bfloat16)
            part = dot(part, pv[level, q], NT)
            total = part if total is None else total + part
        return swap_pairs(total, k)

    value = unpack(recv1[...], rank)
    couplings = []
    for j in range(group_bits):
        level = local_bits + j
        count = group >> j
        couplings.append(coupled(value, level, base >> j, count))
        if level < levels - 1:
            left = every_other(value, k, 0).astype(jnp.bfloat16)
            right = every_other(value, k, 1).astype(jnp.bfloat16)
            value = (dot(left, tv[level, 0], NN) + dot(right, tv[level, 1], NN)) * half_root
            value = value.astype(jnp.bfloat16).astype(jnp.float32)
    outer = []
    for e in range(extra):
        level = local_bits + group_bits + e
        bit = (me // (group << e)) % 2
        outer_send[e] = pack(value, 1)[0]
        copy = pltpu.make_async_remote_copy(
            src_ref=outer_send.at[e],
            dst_ref=outer_recv.at[e],
            send_sem=outer_sems.at[0, e],
            recv_sem=outer_sems.at[1, e],
            device_id=place(outer_partner(e)),
            device_id_type=pl.DeviceIdType.MESH,
        )
        copy.start()
        copy.wait()
        other = unpack(outer_recv[e][None], rank)
        matrix = pv[level, id_at(level, me // (group << e))]
        outer.append(dot(other.astype(jnp.bfloat16), matrix, NT))
        if level < levels - 1:
            own = dot(value.astype(jnp.bfloat16), tv[level, bit], NN)
            value = (own + dot(other.astype(jnp.bfloat16), tv[level, 1 - bit], NN)) * half_root
            value = value.astype(jnp.bfloat16).astype(jnp.float32)

    field = None
    for e in reversed(range(extra)):
        level = local_bits + group_bits + e
        bit = (me // (group << e)) % 2
        below = outer[e]
        if field is not None:
            below += dot(field.astype(jnp.bfloat16), tv[level, bit], NT)
        field = below
    for j in reversed(range(group_bits)):
        level = local_bits + j
        below = couplings[j]
        if field is not None:
            coarse = field.astype(jnp.bfloat16)
            below += interleave(dot(coarse, tv[level, 0], NT), dot(coarse, tv[level, 1], NT), k)
        field = below
    send2[...] = pack(field, group)
    recv2[pl.ds(mine, 1)] = send2[pl.ds(mine, 1)]
    spread(send2, recv2, 2)

    pl.when(not_first)(lambda: halo_copy(0).wait_recv())
    first = pl.ds(0, leaf_rows)
    acc[first, :] += dot(nv[0, 0], halo[0], NN) * mask[0, 0].astype(jnp.float32)
    pl.when(not_last)(lambda: halo_copy(1).wait_recv())
    last = pl.ds((leaf_dev - 1) * leaf_rows, leaf_rows)
    acc[last, :] += dot(nv[leaf_dev - 1, 2], halo[1], NN) * mask[leaf_dev - 1, 1].astype(
        jnp.float32
    )

    settle(recv2, 3)
    fields = [unpack(recv2[...], rank).astype(jnp.bfloat16)]
    for level in reversed(range(local_bits)):
        fields = [
            (loc[starts[level] + a] + dot(fields[a // 2], tv[level, a % 2], NT)).astype(
                jnp.bfloat16
            )
            for a in range(leaf_dev >> level)
        ]
    for i in range(leaf_dev):
        rows = pl.ds(i * leaf_rows, leaf_rows)
        out[rows, :] = (acc[rows, :] + dot(bv[i], fields[i], NT)).astype(out.dtype)

    settle(send1, 0)
    settle(send2, 2)
    pl.when(not_last)(lambda: halo_copy(0).wait_send())
    pl.when(not_first)(lambda: halo_copy(1).wait_send())


def on_device(probes, leaf_basis, transfer, coupling_pool, coupling_ids, near_blocks, near_mask):
    leaf_dev, leaf_rows, rank = leaf_basis.shape
    width = probes.shape[1]
    n_narrow = lax.axis_size("narrow")
    n_wide = lax.axis_size("wide")
    n = n_narrow * n_wide
    group = min(n, width // ROWS)
    extra = (n // group).bit_length() - 1
    panel = (width // group) * rank // LANES
    bf16, f32 = jnp.bfloat16, jnp.float32
    arrays = (
        coupling_ids, near_mask, probes, leaf_basis, transfer, coupling_pool, near_blocks,
    )
    anywhere = pl.BlockSpec(memory_space=pltpu.HBM)
    slots = pltpu.VMEM((group, panel, LANES), bf16)
    outer = pltpu.VMEM((max(extra, 1), panel, LANES), bf16)
    dma = pltpu.SemaphoreType.DMA
    return pl.pallas_call(
        functools.partial(kernel, n_wide, n_narrow, group, extra),
        out_shape=pltpu.VMEM(probes.shape, bf16),
        in_specs=[anywhere] * 7,
        out_specs=pl.BlockSpec(memory_space=pltpu.VMEM),
        scratch_shapes=[
            pltpu.SMEM(coupling_ids.shape, jnp.int32),
            pltpu.SMEM(near_mask.shape, jnp.int32),
            pltpu.VMEM(probes.shape, bf16),
            pltpu.VMEM(leaf_basis.shape, bf16),
            pltpu.VMEM(transfer.shape, bf16),
            pltpu.VMEM((leaf_dev.bit_length() - 1,) + coupling_pool.shape[1:], bf16),
            pltpu.VMEM(coupling_pool.shape, bf16),
            pltpu.VMEM(near_blocks.shape, bf16),
            pltpu.VMEM((2, leaf_rows, width), bf16),
            pltpu.VMEM(probes.shape, f32),
            pltpu.VMEM((2 * leaf_dev - 2, width, rank), bf16),
            pltpu.VMEM((2 * leaf_dev - 2, width, rank), f32),
            slots, slots, slots, slots, outer, outer,
            dma((3 * leaf_dev + 6,)),
            dma((4,)),
            dma((2,)),
            dma((2,)),
            dma((2, max(extra, 1))),
        ],
        compiler_params=pltpu.CompilerParams(
            collective_id=0, has_side_effects=True, vmem_limit_bytes=32 * 1024 * 1024
        ),
    )(*[pltpu.with_memory_space_constraint(array, pltpu.HBM) for array in arrays])


def solution(mesh):
    in_specs = (
        P(("wide", "narrow"), None),
        P(("wide", "narrow"), None, None),
        P(),
        P(),
        P(),
        P(("wide", "narrow"), None, None, None),
        P(("wide", "narrow"), None),
    )
    return jax.shard_map(
        on_device,
        mesh=mesh,
        in_specs=in_specs,
        out_specs=P(("wide", "narrow"), None),
        check_vma=False,
    )
```

```python
import functools

import jax
import jax.numpy as jnp
from jax import lax
from jax.experimental import pallas as pl
from jax.experimental.pallas import tpu as pltpu
from jax.sharding import PartitionSpec as P

half_root = 0.7071067811865476
LANES = 128
ROWS = 8
NN = (((1,), (0,)), ((), ()))
NT = (((1,), (1,)), ((), ()))
TN = (((0,), (0,)), ((), ()))


def dot(a, b, dims):
    return lax.dot_general(a, b, dims, preferred_element_type=jnp.float32)


def pack(value, count):
    rows, rank = value.shape
    parts = [
        value[:, at : at + LANES].reshape(count, rows // count, LANES)
        for at in range(0, rank, LANES)
    ]
    return jnp.concatenate(parts, axis=1).astype(jnp.bfloat16)


def unpack(value, rank):
    count, rows, _ = value.shape
    k = rows * LANES // rank
    value = value.astype(jnp.float32)
    parts = [value[:, at : at + k].reshape(count * k, LANES) for at in range(0, rows, k)]
    return jnp.concatenate(parts, axis=1)


def swap_pairs(value, k):
    rows, rank = value.shape
    blocks = [value[at : at + k] for at in range(0, rows, k)]
    return jnp.concatenate([blocks[b ^ 1] for b in range(rows // k)], axis=0)


def every_other(value, k, first):
    rows, _ = value.shape
    return jnp.concatenate([value[at : at + k] for at in range(first * k, rows, 2 * k)], axis=0)


def interleave(even, odd, k):
    rows, _ = even.shape
    blocks = []
    for at in range(0, rows, k):
        blocks += [even[at : at + k], odd[at : at + k]]
    return jnp.concatenate(blocks, axis=0)


def kernel(
    n_wide, n_narrow, group, extra,
    ids_hbm, mask_hbm, probes, basis, transfer, pool, near, out,
    ids, mask, xv, bv, tv, p_own, pv, nv, halo, acc, joined, coef, loc, send1, recv1, send2, recv2, outer_send, outer_recv,
    load_sem, pair_sem, halo_send, halo_recv, outer_sems,
):
    n = n_wide * n_narrow
    leaf_dev, leaf_rows, rank = bv.shape
    width = xv.shape[1]
    k = width // group
    choices = pv.shape[1]
    local_bits = leaf_dev.bit_length() - 1
    group_bits = group.bit_length() - 1
    levels = local_bits + group_bits + extra
    leaves = leaf_dev * n

    wide, narrow = lax.axis_index("wide"), lax.axis_index("narrow")
    me = wide * n_narrow + narrow
    group_wide = group // n_narrow
    wide_base = wide // group_wide * group_wide if extra else 0
    base = wide_base * n_narrow
    mine = me - base

    def place(device):
        return (device // n_narrow, device % n_narrow)

    def turned(position, step, count):
        moved = position + step
        return jnp.where(moved >= count, moved - count, moved) if step else position

    turns_narrow = []
    for step in range(n_narrow):
        moved = narrow + step
        carried = moved >= n_narrow
        turns_narrow.append((jnp.where(carried, moved - n_narrow, moved), carried))
    turns_wide = [
        turned(wide - wide_base, step % group_wide, group_wide) for step in range(group_wide + 1)
    ]
    others = []
    for step in range(1, group):
        to_narrow, carried = turns_narrow[step % n_narrow]
        at = step // n_narrow
        to_wide = jnp.where(carried, turns_wide[at + 1], turns_wide[at])
        others.append((wide_base + to_wide, to_narrow, to_wide * n_narrow + to_narrow))

    def outer_partner(e):
        stride = group << e
        return me + (1 - 2 * ((me // stride) % 2)) * stride

    def id_at(level, node):
        return ids[2 * leaves - 2 * (leaves >> level) + node]

    loads = {}

    def load(name, src, dst):
        copy = pltpu.make_async_copy(src, dst, load_sem.at[len(loads)])
        copy.start()
        loads[name] = copy

    for i in range(leaf_dev):
        panel = pl.ds(i * leaf_rows, leaf_rows)
        load(("x", i), probes.at[panel], xv.at[panel])
        load(("b", i), basis.at[i], bv.at[i])
    low = pl.ds(0, local_bits)
    high_t = pl.ds(local_bits, levels - 1 - local_bits)
    high_p = pl.ds(local_bits, levels - local_bits)
    load("t_low", transfer.at[low], tv.at[low])
    load("ids", ids_hbm, ids)
    load("mask", mask_hbm, mask)
    load("t_high", transfer.at[high_t], tv.at[high_t])
    load("p_high", pool.at[high_p], pv.at[high_p])
    load("p_low", pool.at[low], p_own)
    for i in range(leaf_dev):
        load(("n", i), near.at[i], nv.at[i])

    barrier = pltpu.get_barrier_semaphore()

    def greet(device_id):
        pl.semaphore_signal(
            barrier, inc=1, device_id=device_id, device_id_type=pl.DeviceIdType.MESH
        )

    for to_wide, to_narrow, _ in others:
        greet((to_wide, to_narrow))
    expected = group - 1
    if extra:
        for e in range(extra):
            greet(place(outer_partner(e)))
        up = jnp.logical_and(mine == group - 1, me < n - 1)
        down = jnp.logical_and(mine == 0, me > 0)
        pl.when(up)(lambda: greet(place(me + 1)))
        pl.when(down)(lambda: greet(place(me - 1)))
        expected = expected + extra + jnp.where(up, 1, 0) + jnp.where(down, 1, 0)

    def panel_of(i):
        return xv[i * leaf_rows : (i + 1) * leaf_rows, :]

    current = []
    for i in range(leaf_dev):
        loads["x", i].wait()
        loads["b", i].wait()
        current.append(dot(panel_of(i), bv[i], TN).astype(jnp.bfloat16))
    loads["t_low"].wait()
    at = 0
    starts = []
    for level in range(local_bits):
        starts.append(at)
        for value in current:
            coef[at] = value
            at += 1
        lifted = [
            (dot(current[2 * a], tv[level, 0], NN) + dot(current[2 * a + 1], tv[level, 1], NN))
            * half_root
            for a in range(len(current) // 2)
        ]
        current = [value.astype(jnp.bfloat16) for value in lifted]
    send1[...] = pack(lifted[0], group)
    recv1[pl.ds(mine, 1)] = send1[pl.ds(mine, 1)]

    loads["p_low"].wait()
    loads["ids"].wait()
    loads["mask"].wait()
    for level in range(local_bits):
        count = leaf_dev >> level
        for a in range(count):
            matrix = p_own[level, id_at(level, me * count + a)]
            loc[starts[level] + a] = dot(coef[starts[level] + (a ^ 1)], matrix, NT)
    for i in range(leaf_dev):
        loads["n", i].wait()
        total = dot(nv[i, 1], panel_of(i), NN)
        if i > 0:
            total += dot(nv[i, 0], panel_of(i - 1), NN) * mask[i, 0].astype(jnp.float32)
        if i < leaf_dev - 1:
            total += dot(nv[i, 2], panel_of(i + 1), NN) * mask[i, 1].astype(jnp.float32)
        acc[i * leaf_rows : (i + 1) * leaf_rows, :] = total
    pl.semaphore_wait(barrier, expected)

    def spread(send, recv, sems):
        for to_wide, to_narrow, to in others:
            pltpu.make_async_remote_copy(
                src_ref=send.at[to],
                dst_ref=recv.at[mine],
                send_sem=pair_sem.at[sems],
                recv_sem=pair_sem.at[sems + 1],
                device_id=(to_wide, to_narrow),
                device_id_type=pl.DeviceIdType.MESH,
            ).start()

    def settle(ref, sem):
        most = ref.at[pl.ds(0, group - 1)]
        pltpu.make_async_copy(most, most, pair_sem.at[sem]).wait()

    spread(send1, recv1, 0)

    def halo_copy(side):
        first = (leaf_dev - 1) * leaf_rows if side == 0 else 0
        return pltpu.make_async_remote_copy(
            src_ref=xv.at[pl.ds(first, leaf_rows)],
            dst_ref=halo.at[side],
            send_sem=halo_send.at[side],
            recv_sem=halo_recv.at[side],
            device_id=place(me + 1 if side == 0 else me - 1),
            device_id_type=pl.DeviceIdType.MESH,
        )

    not_last = me < n - 1
    not_first = me > 0
    pl.when(not_last)(lambda: halo_copy(0).start())
    pl.when(not_first)(lambda: halo_copy(1).start())

    @pl.when(me == 0)
    def _():
        halo[0] = jnp.zeros_like(halo[0])

    @pl.when(me == n - 1)
    def _():
        halo[1] = jnp.zeros_like(halo[1])

    loads["t_high"].wait()
    loads["p_high"].wait()

    settle(recv1, 1)

    def coupled(value, level, first, count):
        chosen = jnp.concatenate(
            [jnp.full((k, rank), id_at(level, first + (b ^ 1)), jnp.int32) for b in range(count)],
            axis=0,
        )
        total = None
        for q in range(choices):
            part = jnp.where(chosen == q, value, 0.0).astype(jnp.bfloat16)
            part = dot(part, pv[level, q], NT)
            total = part if total is None else total + part
        return swap_pairs(total, k)

    value = unpack(recv1[...], rank)
    couplings = []
    for j in range(group_bits):
        level = local_bits + j
        count = group >> j
        couplings.append(coupled(value, level, base >> j, count))
        if level < levels - 1:
            left = every_other(value, k, 0).astype(jnp.bfloat16)
            right = every_other(value, k, 1).astype(jnp.bfloat16)
            value = (dot(left, tv[level, 0], NN) + dot(right, tv[level, 1], NN)) * half_root
            value = value.astype(jnp.bfloat16).astype(jnp.float32)
    outer = []
    for e in range(extra):
        level = local_bits + group_bits + e
        bit = (me // (group << e)) % 2
        outer_send[e] = pack(value, 1)[0]
        copy = pltpu.make_async_remote_copy(
            src_ref=outer_send.at[e],
            dst_ref=outer_recv.at[e],
            send_sem=outer_sems.at[0, e],
            recv_sem=outer_sems.at[1, e],
            device_id=place(outer_partner(e)),
            device_id_type=pl.DeviceIdType.MESH,
        )
        copy.start()
        copy.wait()
        other = unpack(outer_recv[e][None], rank)
        matrix = pv[level, id_at(level, me // (group << e))]
        outer.append(dot(other.astype(jnp.bfloat16), matrix, NT))
        if level < levels - 1:
            own = dot(value.astype(jnp.bfloat16), tv[level, bit], NN)
            value = (own + dot(other.astype(jnp.bfloat16), tv[level, 1 - bit], NN)) * half_root
            value = value.astype(jnp.bfloat16).astype(jnp.float32)

    field = None
    for e in reversed(range(extra)):
        level = local_bits + group_bits + e
        bit = (me // (group << e)) % 2
        below = outer[e]
        if field is not None:
            below += dot(field.astype(jnp.bfloat16), tv[level, bit], NT)
        field = below
    for j in reversed(range(group_bits)):
        level = local_bits + j
        below = couplings[j]
        if field is not None:
            coarse = field.astype(jnp.bfloat16)
            below += interleave(dot(coarse, tv[level, 0], NT), dot(coarse, tv[level, 1], NT), k)
        field = below
    send2[...] = pack(field, group)
    recv2[pl.ds(mine, 1)] = send2[pl.ds(mine, 1)]
    spread(send2, recv2, 2)

    pl.when(not_first)(lambda: halo_copy(0).wait_recv())
    first = pl.ds(0, leaf_rows)
    acc[first, :] += dot(nv[0, 0], halo[0], NN) * mask[0, 0].astype(jnp.float32)
    pl.when(not_last)(lambda: halo_copy(1).wait_recv())
    last = pl.ds((leaf_dev - 1) * leaf_rows, leaf_rows)
    acc[last, :] += dot(nv[leaf_dev - 1, 2], halo[1], NN) * mask[leaf_dev - 1, 1].astype(
        jnp.float32
    )

    for i in range(leaf_dev):
        rows = pl.ds(i * leaf_rows, leaf_rows)
        own = loc[starts[0] + i].astype(jnp.bfloat16)
        acc[rows, :] += dot(bv[i], own, NT)
        joined[i] = dot(bv[i], tv[0, i % 2], NN).astype(jnp.bfloat16)

    settle(recv2, 3)
    fields = [unpack(recv2[...], rank).astype(jnp.bfloat16)]
    for level in reversed(range(1, local_bits)):
        fields = [
            (loc[starts[level] + a] + dot(fields[a // 2], tv[level, a % 2], NT)).astype(
                jnp.bfloat16
            )
            for a in range(leaf_dev >> level)
        ]
    for i in range(leaf_dev):
        rows = pl.ds(i * leaf_rows, leaf_rows)
        out[rows, :] = (acc[rows, :] + dot(joined[i], fields[i // 2], NT)).astype(out.dtype)

    settle(send1, 0)
    settle(send2, 2)
    pl.when(not_last)(lambda: halo_copy(0).wait_send())
    pl.when(not_first)(lambda: halo_copy(1).wait_send())


def on_device(probes, leaf_basis, transfer, coupling_pool, coupling_ids, near_blocks, near_mask):
    leaf_dev, leaf_rows, rank = leaf_basis.shape
    width = probes.shape[1]
    n_narrow = lax.axis_size("narrow")
    n_wide = lax.axis_size("wide")
    n = n_narrow * n_wide
    group = min(n, width // ROWS)
    extra = (n // group).bit_length() - 1
    panel = (width // group) * rank // LANES
    bf16, f32 = jnp.bfloat16, jnp.float32
    arrays = (
        coupling_ids, near_mask, probes, leaf_basis, transfer, coupling_pool, near_blocks,
    )
    anywhere = pl.BlockSpec(memory_space=pltpu.HBM)
    slots = pltpu.VMEM((group, panel, LANES), bf16)
    outer = pltpu.VMEM((max(extra, 1), panel, LANES), bf16)
    dma = pltpu.SemaphoreType.DMA
    return pl.pallas_call(
        functools.partial(kernel, n_wide, n_narrow, group, extra),
        out_shape=pltpu.VMEM(probes.shape, bf16),
        in_specs=[anywhere] * 7,
        out_specs=pl.BlockSpec(memory_space=pltpu.VMEM),
        scratch_shapes=[
            pltpu.SMEM(coupling_ids.shape, jnp.int32),
            pltpu.SMEM(near_mask.shape, jnp.int32),
            pltpu.VMEM(probes.shape, bf16),
            pltpu.VMEM(leaf_basis.shape, bf16),
            pltpu.VMEM(transfer.shape, bf16),
            pltpu.VMEM((leaf_dev.bit_length() - 1,) + coupling_pool.shape[1:], bf16),
            pltpu.VMEM(coupling_pool.shape, bf16),
            pltpu.VMEM(near_blocks.shape, bf16),
            pltpu.VMEM((2, leaf_rows, width), bf16),
            pltpu.VMEM(probes.shape, f32),
            pltpu.VMEM(leaf_basis.shape, bf16),
            pltpu.VMEM((2 * leaf_dev - 2, width, rank), bf16),
            pltpu.VMEM((2 * leaf_dev - 2, width, rank), f32),
            slots, slots, slots, slots, outer, outer,
            dma((3 * leaf_dev + 6,)),
            dma((4,)),
            dma((2,)),
            dma((2,)),
            dma((2, max(extra, 1))),
        ],
        compiler_params=pltpu.CompilerParams(
            collective_id=0, has_side_effects=True, vmem_limit_bytes=32 * 1024 * 1024
        ),
    )(*[pltpu.with_memory_space_constraint(array, pltpu.HBM) for array in arrays])


def solution(mesh):
    in_specs = (
        P(("wide", "narrow"), None),
        P(("wide", "narrow"), None, None),
        P(),
        P(),
        P(),
        P(("wide", "narrow"), None, None, None),
        P(("wide", "narrow"), None),
    )
    return jax.shard_map(
        on_device,
        mesh=mesh,
        in_specs=in_specs,
        out_specs=P(("wide", "narrow"), None),
        check_vma=False,
    )
```
